32 devices in a mesh: leaf: 4 (over z), row: 2 (over y), col: 4 (over x, core).
Axes of the slice: x: 2, y: 2, z: 4, core: 2. Of those that a mesh axis runs over, the one named last changes fastest.
Arguments:
- rhs_root: bfloat16 [64, 4, 768], P('col', None, ('leaf', 'row')), may hold values from -6 to 6
- rhs_child: bfloat16 [64, 4, 768], P('col', None, ('leaf', 'row')), may hold values from -6 to 6
- subtree_update: bfloat16 [64, 4, 1024], P('col', None, ('leaf', 'row')), may hold values from -6 to 6
- inv_root: bfloat16 [4, 768, 3072], P(None, ('leaf', 'row'), 'col'), as said below
- inv_child: bfloat16 [4, 768, 1536], P(None, ('leaf', 'row'), 'col'), as said below
- off_child: bfloat16 [4, 1024, 1536], P(None, ('leaf', 'row'), 'col'), may hold values from -0.15625 to 0.15625
- child_map: int32 [2, 16], replicated, may hold values from 0 to 23, as said below
- subtree_map: int32 [4, 8], replicated, may hold values from 0 to 27, as said below
Outputs:
- solution_root: float32 [64, 4, 768], P('col', None, ('leaf', 'row'))
- solution_child: float32 [64, 4, 768], P('col', None, ('leaf', 'row'))
- leaf_solution: bfloat16 [64, 4, 1024], P('col', None, ('leaf', 'row'))
The draws below stay inside these ranges and needn't reach their ends.
Inputs may be any that keep to these rules, and one draw needn't show every extreme that they name: `child_map`: each row names 16 different blocks. `subtree_map`: each row names 8 different blocks. `inv_root`: zero above the diagonal, positive on it. `inv_child`: each child's block is zero above the diagonal, positive on it.
All inputs are finite; a program needn't handle non-finite values.
Results may differ from the reference program's by a relative error of at most 0.017.
Values may be sent and summed in bfloat16 or wider, within the bound.
A program may use at most 64 MiB of HBM per device.

```python
import math
import jax
import jax.numpy as jnp
from jax import lax

RIGHT_SIDES = 64
BLOCK_ROWS = 128
ROOT_ORDER = 3072
CHILD_ORDER = 1536
CHILD_UPDATE = 2048
SUBTREE_UPDATE = 1024
ROOT_BLOCKS = 24
CHILD_BLOCKS = 28
UPDATE_BLOCKS = 16
SUBTREE_BLOCKS = 8
N_COL = 4


def triangle(key, row_number, column_number, order):
    first_key, second_key = jax.random.split(key)
    extent = row_number.shape
    spread = jnp.clip(jax.random.normal(first_key, extent, jnp.float32), -6.0, 6.0)
    diagonal = jax.random.uniform(second_key, extent, jnp.float32, 0.5, 1.5)
    lower_part = spread / math.sqrt(order)
    return jnp.where(column_number < row_number, lower_part, jnp.where(column_number == row_number, diagonal, 0.0))


def draw_inv_root(key, part):
    extent = (N_COL, ROOT_ORDER // N_COL, ROOT_ORDER)
    quarter = lax.broadcasted_iota(jnp.int32, extent, 0)
    within = lax.broadcasted_iota(jnp.int32, extent, 1)
    column_number = lax.broadcasted_iota(jnp.int32, extent, 2)
    row_number = quarter * (ROOT_ORDER // N_COL) + within
    return triangle(key, row_number, column_number, ROOT_ORDER).astype(jnp.bfloat16)


def draw_inv_child(key, part):
    extent = (N_COL, 2 * CHILD_ORDER // N_COL, CHILD_ORDER)
    quarter = lax.broadcasted_iota(jnp.int32, extent, 0)
    within = lax.broadcasted_iota(jnp.int32, extent, 1) % (CHILD_ORDER // N_COL)
    column_number = lax.broadcasted_iota(jnp.int32, extent, 2)
    row_number = quarter * (CHILD_ORDER // N_COL) + within
    return triangle(key, row_number, column_number, CHILD_ORDER).astype(jnp.bfloat16)


def block_table(key, table_rows, width_blocks, limit):
    table = []
    for number in range(table_rows):
        row_key = jax.random.fold_in(key, number)
        if number == 0:
            middle = 1 + jax.random.permutation(row_key, limit - 2)[:width_blocks - 2]
            edges = jnp.array([0, limit - 1], dtype=jnp.int32)
            entries = jax.random.permutation(jax.random.fold_in(row_key, 101), jnp.concatenate([edges, middle.astype(jnp.int32)]))
        else:
            entries = jax.random.permutation(row_key, limit)[:width_blocks]
        table.append(entries.astype(jnp.int32))
    return jnp.stack(table)


def draw_child_map(key, part):
    return block_table(key, 2, UPDATE_BLOCKS, ROOT_BLOCKS)


def draw_subtree_map(key, part):
    return block_table(key, 4, SUBTREE_BLOCKS, CHILD_BLOCKS)


def level_of(own_key, shape, cuts, low, top_value):
    level = 1.0
    for position, blocks in cuts:
        steps = jax.random.uniform(jax.random.fold_in(jax.random.fold_in(own_key, 6), position), (blocks,), jnp.float32, low / len(cuts), top_value / len(cuts))
        level = level * jnp.repeat(jnp.exp(steps), shape[position] // blocks).reshape((-1,) + (1,) * (len(shape) - 1 - position))
    return level


def gaussian(own_key, shape, deviation, most, cuts=(), held_as=jnp.bfloat16):
    level = level_of(own_key, shape, cuts, -0.22, 0.18) if cuts else 1.0
    values = jax.random.normal(own_key, shape, jnp.float32) * deviation * level
    return jnp.minimum(jnp.maximum(values, -most), most).astype(held_as)


def setup_inputs(seed: int = 0) -> dict:
    seeds = jax.random.split(jax.random.key(seed), 9)
    return {
        "rhs_root": gaussian(seeds[0], (RIGHT_SIDES, N_COL, ROOT_ORDER // N_COL), 1.0, 6.0, ((0, 4), (2, 8))),
        "rhs_child": gaussian(seeds[1], (RIGHT_SIDES, N_COL, 2 * CHILD_ORDER // N_COL), 1.0, 6.0, ((0, 4), (2, 8))),
        "subtree_update": gaussian(seeds[2], (RIGHT_SIDES, N_COL, 4 * SUBTREE_UPDATE // N_COL), 1.0, 6.0, ((0, 4), (2, 8))),
        "inv_root": draw_inv_root(jax.random.fold_in(seeds[8], 71), 0),
        "inv_child": draw_inv_child(jax.random.fold_in(seeds[8], 71), 0),
        "off_child": gaussian(seeds[5], (N_COL, 2 * CHILD_UPDATE // N_COL, CHILD_ORDER), CHILD_ORDER ** -0.5, 0.15625, ((1, 8), (2, 4))),
        "child_map": draw_child_map(jax.random.fold_in(seeds[8], 71), 0),
        "subtree_map": draw_subtree_map(jax.random.fold_in(seeds[8], 71), 0),
    }


def add_blocks(front_vector, update, block_map):
    right_sides = front_vector.shape[0]
    blocks = front_vector.reshape(right_sides, -1, BLOCK_ROWS)
    pieces = update.astype(jnp.float32).reshape(right_sides, -1, BLOCK_ROWS)
    return blocks.at[:, block_map, :].add(pieces).reshape(right_sides, -1)


def pick_blocks(front_vector, block_map):
    right_sides = front_vector.shape[0]
    return front_vector.reshape(right_sides, -1, BLOCK_ROWS)[:, block_map, :].reshape(right_sides, -1)


def unpack_vectors(packed, fronts):
    right_sides, tile_count, length = packed.shape
    return packed.reshape(right_sides, tile_count, fronts, length // fronts).transpose(2, 0, 1, 3).reshape(fronts, right_sides, -1)


def pack_vectors(stacked):
    fronts, right_sides, length = stacked.shape
    return stacked.reshape(fronts, right_sides, N_COL, length // N_COL).transpose(1, 2, 0, 3).reshape(right_sides, N_COL, -1)


def unpack_blocks(packed, fronts):
    tile_count, height, columns_all = packed.shape
    return packed.reshape(tile_count, fronts, height // fronts, columns_all).transpose(1, 0, 2, 3).reshape(fronts, -1, columns_all)


def reference(rhs_root, rhs_child, subtree_update, inv_root, inv_child, off_child, child_map, subtree_map):
    root_order = inv_root.shape[2]
    child_order = inv_child.shape[2]
    root_matrix = inv_root.reshape(root_order, root_order)
    child_matrices = unpack_blocks(inv_child, 2)
    off_matrices = unpack_blocks(off_child, 2)
    child_update = off_matrices.shape[1]
    right_sides = rhs_root.shape[0]
    child_rhs = unpack_vectors(rhs_child, 2)
    subtree_vectors = unpack_vectors(subtree_update, 4)
    forwards = []
    passes = []
    for front_number in range(2):
        front_vector = jnp.concatenate([child_rhs[front_number].astype(jnp.float32), jnp.zeros((right_sides, child_update), jnp.float32)], 1)
        for half_number in range(2):
            subtree_number = 2 * front_number + half_number
            front_vector = add_blocks(front_vector, subtree_vectors[subtree_number], subtree_map[subtree_number])
        separator = front_vector[:, :child_order].astype(jnp.bfloat16)
        forward = jnp.dot(separator, child_matrices[front_number].T, preferred_element_type=jnp.float32).astype(jnp.bfloat16)
        passed = (front_vector[:, child_order:] - jnp.dot(forward, off_matrices[front_number].T, preferred_element_type=jnp.float32)).astype(jnp.bfloat16)
        forwards.append(forward)
        passes.append(passed)
    root_vector = rhs_root.reshape(right_sides, root_order).astype(jnp.float32)
    for front_number in range(2):
        root_vector = add_blocks(root_vector, passes[front_number], child_map[front_number])
    root_forward = jnp.dot(root_vector.astype(jnp.bfloat16), root_matrix.T, preferred_element_type=jnp.float32).astype(jnp.bfloat16)
    solution_root = jnp.dot(root_forward, root_matrix, preferred_element_type=jnp.float32)
    root_rounded = solution_root.astype(jnp.bfloat16)
    solutions = []
    leaves = []
    for front_number in range(2):
        known_rows = pick_blocks(root_rounded, child_map[front_number])
        backward = (forwards[front_number].astype(jnp.float32) - jnp.dot(known_rows, off_matrices[front_number], preferred_element_type=jnp.float32)).astype(jnp.bfloat16)
        solution = jnp.dot(backward, child_matrices[front_number], preferred_element_type=jnp.float32)
        whole_front = jnp.concatenate([solution.astype(jnp.bfloat16), known_rows], 1)
        solutions.append(solution)
        for half_number in range(2):
            leaves.append(pick_blocks(whole_front, subtree_map[2 * front_number + half_number]))
    return (solution_root.reshape(right_sides, N_COL, root_order // N_COL), pack_vectors(jnp.stack(solutions)), pack_vectors(jnp.stack(leaves)))
```

```python
import functools

import jax
import jax.numpy as jnp
from jax import lax
from jax.experimental import pallas as pl
from jax.experimental.pallas import tpu as pltpu
from jax.sharding import PartitionSpec as P

BLOCK_ROWS = 128


def partner_2(block, axis, bit):
    count = lax.axis_size(axis)
    route = []
    for low in range(count):
        high = low | 1 << bit
        if high != low and high < count:
            route += [(low, high), (high, low)]
    return lax.ppermute(block, axis, route)


def group_gather(piece, group_size):
    merged = lax.all_gather(piece, "row", axis=2, tiled=True)
    leaf_index = lax.axis_index("leaf")
    for bit_number in range(group_size.bit_length() - 1):
        partner = partner_2(merged, "leaf", bit_number)
        upper = leaf_index >> bit_number & 1 == 1
        merged = jnp.where(
            upper, jnp.concatenate([partner, merged], 2), jnp.concatenate([merged, partner], 2)
        )
    return merged


def group_sum(partial_sum, group_size):
    leaf_index = lax.axis_index("leaf")
    for bit_number in reversed(range(group_size.bit_length() - 1)):
        middle = partial_sum.shape[1] // 2
        lower_half = partial_sum[:, :middle]
        upper_half = partial_sum[:, middle:]
        upper = leaf_index >> bit_number & 1 == 1
        outgoing = jnp.where(upper, lower_half, upper_half)
        kept_half = jnp.where(upper, upper_half, lower_half)
        partial_sum = kept_half + partner_2(
            outgoing.astype(jnp.bfloat16), "leaf", bit_number
        ).astype(outgoing.dtype)
    return lax.psum_scatter(
        partial_sum.astype(jnp.bfloat16), "row", scatter_dimension=1, tiled=True
    ).astype(jnp.float32)


def one_hot(block_map, blocks_total):
    return (block_map[..., None] == jnp.arange(blocks_total, dtype=jnp.int32)).astype(jnp.bfloat16)


def pick_piece(source, position, along):
    return lax.dynamic_index_in_dim(source, position, along, keepdims=False)


def contract(left_side, right_side, left_dim, right_dim):
    return lax.dot_general(
        left_side,
        right_side,
        (((left_dim,), (right_dim,)), ((), ())),
        preferred_element_type=jnp.float32,
    )


def local(
    rhs_root, rhs_child, subtree_update, inv_root, inv_child, off_child, child_map, subtree_map
):
    n_col = lax.axis_size("col")
    n_row = lax.axis_size("row")
    n_leaf = lax.axis_size("leaf")
    group_size = n_leaf // 2
    sub_size = n_leaf // 4
    col_index = lax.axis_index("col")
    leaf_index = lax.axis_index("leaf")
    row_index = lax.axis_index("row")
    front_index = leaf_index // group_size
    member = leaf_index % group_size
    child_rank = member * n_row + row_index
    half_index = member // sub_size
    sub_rank = member % sub_size * n_row + row_index
    panel_width = rhs_child.shape[0]
    right_sides = panel_width * n_col
    sep_piece = rhs_child.shape[2]
    upd_piece = subtree_update.shape[2]
    root_width = inv_root.shape[2]
    child_width = inv_child.shape[2]
    child_order = child_width * n_col
    child_update = upd_piece * n_col * group_size * n_row
    root_blocks = root_width * n_col // BLOCK_ROWS
    child_blocks = (child_order + child_update) // BLOCK_ROWS
    root_matrix = inv_root.reshape(n_col * sep_piece, root_width)
    child_matrix = inv_child.reshape(n_col * sep_piece, child_width)
    off_matrix = off_child.reshape(n_col * upd_piece, child_width)
    joined = jnp.concatenate([subtree_update, rhs_child], 2)
    gathered = group_gather(joined, group_size).reshape(
        panel_width, n_col, group_size * n_row, upd_piece + sep_piece
    )
    sub_vectors = (
        gathered[..., :upd_piece]
        .reshape(panel_width, n_col, 2, -1)
        .transpose(2, 0, 1, 3)
        .reshape(2, panel_width, -1, BLOCK_ROWS)
    )
    child_rhs_full = gathered[..., upd_piece:].reshape(panel_width, child_order)
    sub_rows = lax.dynamic_slice_in_dim(subtree_map, 2 * front_index, 2, 0)
    spread = jnp.einsum(
        "hpjt,hjn->pnt",
        sub_vectors,
        one_hot(sub_rows, child_blocks),
        preferred_element_type=jnp.float32,
    ).reshape(panel_width, -1)
    child_sep = (spread[:, :child_order] + child_rhs_full.astype(jnp.float32)).astype(jnp.bfloat16)
    child_tail = spread[:, child_order:]
    child_tile = lax.all_to_all(
        child_sep.reshape(panel_width, n_col, child_width),
        "col",
        split_axis=1,
        concat_axis=0,
        tiled=True,
    ).reshape(right_sides, child_width)
    child_forward = lax.psum(contract(child_tile, child_matrix, 1, 1), "col").astype(jnp.bfloat16)
    forward_quarter = lax.dynamic_slice_in_dim(
        child_forward.reshape(right_sides, n_col, sep_piece), col_index, 1, 1
    )
    forward_tile = group_gather(forward_quarter, group_size).reshape(right_sides, child_width)
    pass_term = lax.psum_scatter(
        contract(forward_tile, off_matrix, 1, 1), "col", scatter_dimension=0, tiled=True
    )
    tail_mine = pick_piece(
        child_tail.reshape(panel_width, n_col, group_size * n_row, upd_piece), child_rank, 2
    )
    child_pass = (tail_mine - pass_term.reshape(panel_width, n_col, upd_piece)).astype(jnp.bfloat16)
    joined_root = jnp.concatenate([child_pass, rhs_root], 2)
    root_all = lax.all_gather(joined_root, ("leaf", "row"), axis=2, tiled=True).reshape(
        panel_width, n_col, n_leaf * n_row, upd_piece + sep_piece
    )
    pass_vectors = (
        root_all[..., :upd_piece]
        .reshape(panel_width, n_col, 2, -1)
        .transpose(2, 0, 1, 3)
        .reshape(2, panel_width, -1, BLOCK_ROWS)
    )
    root_rhs_full = root_all[..., upd_piece:].reshape(panel_width, root_width * n_col)
    root_spread = jnp.einsum(
        "hpjt,hjn->pnt",
        pass_vectors,
        one_hot(child_map, root_blocks),
        preferred_element_type=jnp.float32,
    ).reshape(panel_width, -1)
    root_sep = (root_spread + root_rhs_full.astype(jnp.float32)).astype(jnp.bfloat16)
    root_tile = lax.all_to_all(
        root_sep.reshape(panel_width, n_col, root_width),
        "col",
        split_axis=1,
        concat_axis=0,
        tiled=True,
    ).reshape(right_sides, root_width)
    root_forward = lax.psum(contract(root_tile, root_matrix, 1, 1), "col").astype(jnp.bfloat16)
    map_row = pick_piece(child_map, front_index, 0)
    root_piece = lax.psum_scatter(
        contract(root_matrix, root_forward, 0, 1), ("leaf", "row"), scatter_dimension=0, tiled=True
    )
    solution_root = lax.all_to_all(
        root_piece.T.reshape(right_sides, 1, sep_piece),
        "col",
        split_axis=0,
        concat_axis=1,
        tiled=True,
    )
    root_everywhere = lax.all_gather(
        solution_root.astype(jnp.bfloat16), ("leaf", "row"), axis=2, tiled=True
    ).reshape(panel_width, root_blocks, BLOCK_ROWS)
    known_full = (
        jnp.einsum(
            "pnt,jn->pjt",
            root_everywhere,
            one_hot(map_row, root_blocks),
            preferred_element_type=jnp.float32,
        )
        .astype(jnp.bfloat16)
        .reshape(panel_width, child_update)
    )
    known_mine = pick_piece(
        known_full.reshape(panel_width, n_col, group_size * n_row, upd_piece), child_rank, 2
    )
    known_rows = lax.all_gather(known_mine, "col", axis=0, tiled=True).reshape(
        right_sides, n_col * upd_piece
    )
    correction = group_sum(contract(known_rows, off_matrix, 1, 0), group_size)
    back_quarter = (
        forward_quarter.reshape(right_sides, sep_piece).astype(jnp.float32) - correction
    ).astype(jnp.bfloat16)
    back_rows = lax.all_gather(
        back_quarter.reshape(right_sides, 1, sep_piece), "col", axis=1, tiled=True
    ).reshape(right_sides, n_col * sep_piece)
    child_piece = group_sum(contract(back_rows, child_matrix, 1, 0), group_size)
    solution_child = lax.all_to_all(
        child_piece.reshape(right_sides, 1, sep_piece),
        "col",
        split_axis=0,
        concat_axis=1,
        tiled=True,
    )
    child_rounded = solution_child.astype(jnp.bfloat16)
    sep_whole = group_gather(child_rounded, group_size).reshape(panel_width, child_order)
    child_whole = jnp.concatenate([sep_whole, known_full], 1)
    sub_row = pick_piece(subtree_map, 2 * front_index + half_index, 0)
    leaf_full = jnp.einsum(
        "pnt,jn->pjt",
        child_whole.reshape(panel_width, child_blocks, BLOCK_ROWS),
        one_hot(sub_row, child_blocks),
        preferred_element_type=jnp.float32,
    ).astype(jnp.bfloat16)
    leaf_solution = pick_piece(
        leaf_full.reshape(panel_width, n_col, sub_size * n_row, upd_piece), sub_rank, 2
    )
    return (solution_root, solution_child, leaf_solution)


F32 = jnp.float32
BF16 = jnp.bfloat16


def inverse_table(block_map, blocks_total, places):
    hit = block_map[..., None] == jnp.arange(blocks_total, dtype=jnp.int32)
    return jnp.sum(jnp.where(hit, places[:, None] + 1, 0), axis=-2, dtype=jnp.int32) - 1


def add_up(terms):
    total = terms[0]
    for term in terms[1:]:
        total = total + term
    return total


def solve_kernel(
    dims,
    sub_table, root_table, leaf_table, child_map,
    sub_in, rc_in, rr_in, root_hbm, child_hbm, off_hbm,
    root_out, child_out, leaf_out,
    root_w, child_w, off_w,
    sub_buf, rc_buf, rr_buf,
    p2_send, p2_recv, p3_send, p3_recv, pass_send, pass_buf,
    tile_send, tile_recv, p4_send, p4_recv, p5_send, p5_recv,
    sr_send, sr_recv, kn_send, kn_recv, p7_send, p7_recv, p8_send, p8_recv,
    blocks, pieces,
    load_sems, send_sems, recv_sems,
):
    n_leaf, n_row, n_col = dims
    panel = sub_in.shape[1]
    sep = rc_in.shape[2]
    ranks = n_row * (n_leaf // 2)
    rows_all = n_leaf * n_row
    group = ranks * n_col
    everyone = rows_all * n_col
    right = panel * n_col
    child_tile_blocks = child_w.shape[2] // BLOCK_ROWS
    root_tile_blocks = root_w.shape[2] // BLOCK_ROWS
    sep_blocks = child_tile_blocks * n_col
    c = lax.axis_index("col")
    leaf = lax.axis_index("leaf")
    row = lax.axis_index("row")
    half = n_leaf // 2
    front = lax.div(leaf, half)
    rank = lax.rem(leaf, half) * n_row + row
    r = leaf * n_row + row
    gid = c * ranks + rank
    me = r * n_col + c

    loads = [
        pltpu.make_async_copy(child_hbm, child_w, load_sems.at[0]),
        pltpu.make_async_copy(off_hbm, off_w, load_sems.at[1]),
        pltpu.make_async_copy(root_hbm, root_w, load_sems.at[2]),
    ]
    for load in loads:
        load.start()

    def at_row(r2, c2):
        return {"leaf": lax.div(r2, n_row), "row": lax.rem(r2, n_row), "col": c2}

    def at_group(g2):
        return at_row(front * ranks + lax.rem(g2, ranks), lax.div(g2, ranks))

    def each(count, own, body):
        def step(k, carry):
            body(lax.rem(own + k, count))
            return carry

        lax.fori_loop(1, count, step, 0)

    def push(source, target, phase, device):
        pltpu.make_async_remote_copy(
            src_ref=source,
            dst_ref=target,
            send_sem=send_sems.at[phase],
            recv_sem=recv_sems.at[phase],
            device_id=device,
            device_id_type=pl.DeviceIdType.MESH,
        ).start()

    def drain(view, sem):
        pltpu.make_async_copy(view, view, sem).wait()

    barrier = pltpu.get_barrier_semaphore()

    def greet(d):
        pl.semaphore_signal(
            barrier, inc=1, device_id=at_row(lax.div(d, n_col), lax.rem(d, n_col)),
            device_id_type=pl.DeviceIdType.MESH,
        )

    each(everyone, me, greet)
    pl.semaphore_wait(barrier, everyone - 1)

    each(group, gid, lambda g2: push(rc_in.at[lax.div(g2, ranks)], rc_buf.at[gid], 1, at_group(g2)))
    each(group, gid, lambda g2: push(sub_in, sub_buf.at[pl.ds(gid * n_col, n_col)], 0, at_group(g2)))
    each(rows_all, r, lambda r2: push(rr_in, rr_buf.at[r], 2, at_row(r2, c)))
    sub_buf[pl.ds(gid * n_col, n_col)] = sub_in[...]
    rc_buf[gid] = rc_in[c]
    rr_buf[r] = rr_in[...]
    loads[0].wait()
    drain(rc_buf.at[pl.ds(0, group - 1)], recv_sems.at[1])
    drain(sub_buf.at[pl.ds(0, (group - 1) * n_col)], recv_sems.at[0])

    def placed(p, block):
        total = None
        for h in range(2):
            place = sub_table[2 * front + h, block]
            value = sub_buf[p * ranks * n_col + jnp.maximum(place, 0)].astype(F32)
            value = jnp.where(place >= 0, value, jnp.zeros_like(value))
            total = value if total is None else total + value
        return total

    def rows_of(values):
        return jnp.concatenate(values, 0)

    x = jnp.concatenate(
        [rows_of([rc_buf[p * ranks + k] for p in range(n_col)]).astype(F32) for k in range(ranks)], 1
    )
    x = x + jnp.concatenate(
        [
            rows_of([placed(p, c * child_tile_blocks + b) for p in range(n_col)])
            for b in range(child_tile_blocks)
        ],
        1,
    )
    x = x.astype(BF16)
    for q in range(n_col):
        p2_send[q] = contract(x, child_w[q], 1, 1).astype(BF16)

    each(group, gid, lambda g2: push(p2_send.at[lax.div(g2, ranks)], p2_recv.at[gid], 3, at_group(g2)))
    p2_recv[gid] = p2_send[c]
    tail = [placed(c, sep_blocks + q * ranks + rank) for q in range(n_col)]
    loads[1].wait()
    drain(p2_recv.at[pl.ds(0, group - 1)], recv_sems.at[3])
    forward = [
        add_up([p2_recv[c2 * ranks + k].astype(F32) for c2 in range(n_col)]).astype(BF16)
        for k in range(ranks)
    ]
    y = jnp.concatenate([piece.astype(F32) for piece in forward], 1).astype(BF16)
    for q in range(n_col):
        z = contract(y, off_w[q], 1, 1).astype(BF16)
        for p in range(n_col):
            p3_send[p, q] = z[p * panel : (p + 1) * panel]

    each(n_col, c, lambda c2: push(p3_send.at[c2], p3_recv.at[c], 4, at_row(r, c2)))
    p3_recv[c] = p3_send[c]
    drain(p3_recv.at[pl.ds(0, n_col - 1)], recv_sems.at[4])
    for q in range(n_col):
        total = add_up([p3_recv[c2, q].astype(F32) for c2 in range(n_col)])
        pass_send[q] = (tail[q] - total).astype(BF16)

    each(rows_all, r, lambda r2: push(pass_send, pass_buf.at[pl.ds(r * n_col, n_col)], 5, at_row(r2, c)))
    pass_buf[pl.ds(r * n_col, n_col)] = pass_send[...]
    drain(rr_buf.at[pl.ds(0, rows_all - 1)], recv_sems.at[2])
    x = jnp.concatenate(
        [rr_buf[k].reshape(right, sep).astype(F32) for k in range(rows_all)], 1
    )
    drain(pass_buf.at[pl.ds(0, (rows_all - 1) * n_col)], recv_sems.at[5])

    def passed(block):
        total = None
        for f in range(2):
            place = root_table[f, block]
            value = pass_buf[jnp.maximum(place, 0)].astype(F32)
            value = jnp.where(place >= 0, value, jnp.zeros_like(value))
            total = value if total is None else total + value
        return total

    x = x + jnp.concatenate(
        [
            rows_of([passed(q * root_tile_blocks + b) for q in range(n_col)])
            for b in range(root_tile_blocks)
        ],
        1,
    )
    tile_send[...] = x.astype(BF16).reshape(tile_send.shape)

    each(n_col, c, lambda c2: push(tile_send.at[c2], tile_recv.at[c], 6, at_row(r, c2)))
    tile_recv[c] = tile_send[c]
    loads[2].wait()
    drain(tile_recv.at[pl.ds(0, n_col - 1)], recv_sems.at[6])
    x = tile_recv[...].reshape(right, root_w.shape[2])
    for q in range(n_col):
        p4_send[q] = contract(x, root_w[q], 1, 1).astype(BF16)

    each(n_col, c, lambda c2: push(p4_send, p4_recv.at[c], 7, at_row(r, c2)))
    p4_recv[c] = p4_send[...]
    drain(p4_recv.at[pl.ds(0, n_col - 1)], recv_sems.at[7])
    total = None
    for q in range(n_col):
        piece = add_up([p4_recv[c2, q].astype(F32) for c2 in range(n_col)]).astype(BF16)
        term = contract(piece, root_w[q], 1, 0)
        total = term if total is None else total + term
    for r2 in range(rows_all):
        piece = total[:, r2 * sep : (r2 + 1) * sep].astype(BF16)
        for p in range(n_col):
            p5_send[r2 * n_col + p] = piece[p * panel : (p + 1) * panel]

    each(
        everyone, me,
        lambda d: push(
            p5_send.at[d], p5_recv.at[c * rows_all + r], 8,
            at_row(lax.div(d, n_col), lax.rem(d, n_col)),
        ),
    )
    p5_recv[c * rows_all + r] = p5_send[me]
    drain(p5_recv.at[pl.ds(0, everyone - 1)], recv_sems.at[8])
    for q in range(n_col):
        total = add_up([p5_recv[q * rows_all + k].astype(F32) for k in range(rows_all)])
        root_out[q] = total
        sr_send[q] = total.astype(BF16)

    each(rows_all, r, lambda r2: push(sr_send, sr_recv.at[r], 9, at_row(r2, c)))
    sr_recv[r] = sr_send[...]
    drain(sr_recv.at[pl.ds(0, rows_all - 1)], recv_sems.at[9])
    x = jnp.concatenate(
        [sr_recv[k].reshape(right, sep).astype(F32) for k in range(rows_all)], 1
    ).astype(BF16)
    for q in range(n_col):
        for b in range(root_tile_blocks):
            blocks[sep_blocks + q * root_tile_blocks + b] = x[
                q * panel : (q + 1) * panel, b * BLOCK_ROWS : (b + 1) * BLOCK_ROWS
            ]
    for q in range(n_col):
        kn_send[q] = blocks[sep_blocks + child_map[front, q * ranks + rank]]

    each(n_col, c, lambda c2: push(kn_send, kn_recv.at[c], 10, at_row(r, c2)))
    kn_recv[c] = kn_send[...]
    drain(kn_recv.at[pl.ds(0, n_col - 1)], recv_sems.at[10])
    total = None
    for q in range(n_col):
        term = contract(rows_of([kn_recv[p, q] for p in range(n_col)]), off_w[q], 1, 0)
        total = term if total is None else total + term
    for k in range(ranks):
        own = jnp.where(rank == k, forward[k].astype(F32), jnp.zeros(forward[k].shape, F32))
        p7_send[k] = (own - total[:, k * sep : (k + 1) * sep]).astype(BF16)

    each(group, gid, lambda g2: push(p7_send.at[lax.rem(g2, ranks)], p7_recv.at[gid], 11, at_group(g2)))
    p7_recv[gid] = p7_send[rank]
    drain(p7_recv.at[pl.ds(0, group - 1)], recv_sems.at[11])
    total = None
    for q in range(n_col):
        piece = add_up([p7_recv[q * ranks + k].astype(F32) for k in range(ranks)]).astype(BF16)
        term = contract(piece, child_w[q], 1, 0)
        total = term if total is None else total + term
    p8_send[...] = total.astype(BF16).reshape(p8_send.shape)

    each(group, gid, lambda g2: push(p8_send.at[lax.div(g2, ranks)], p8_recv.at[gid], 12, at_group(g2)))
    p8_recv[gid] = p8_send[c]
    drain(p8_recv.at[pl.ds(0, group - 1)], recv_sems.at[12])
    for q in range(n_col):
        total = add_up([p8_recv[q * ranks + k].astype(F32) for k in range(ranks)])
        for k in range(ranks):
            pieces[q, k] = total[:, k * sep : (k + 1) * sep]
        child_out[q] = pieces[q, rank]
        total = total.astype(BF16)
        for b in range(child_tile_blocks):
            blocks[q * child_tile_blocks + b] = total[:, b * BLOCK_ROWS : (b + 1) * BLOCK_ROWS]
    for q in range(n_col):
        leaf_out[q] = blocks[leaf_table[leaf, q * n_row + row]]

    drain(rc_buf.at[pl.ds(0, group - 1)], send_sems.at[1])
    drain(sub_buf.at[pl.ds(0, (group - 1) * n_col)], send_sems.at[0])
    drain(rr_buf.at[pl.ds(0, rows_all - 1)], send_sems.at[2])
    drain(p2_recv.at[pl.ds(0, group - 1)], send_sems.at[3])
    drain(p3_recv.at[pl.ds(0, n_col - 1)], send_sems.at[4])
    drain(pass_buf.at[pl.ds(0, (rows_all - 1) * n_col)], send_sems.at[5])
    drain(tile_recv.at[pl.ds(0, n_col - 1)], send_sems.at[6])
    drain(p4_recv.at[pl.ds(0, n_col - 1)], send_sems.at[7])
    drain(p5_recv.at[pl.ds(0, everyone - 1)], send_sems.at[8])
    drain(sr_recv.at[pl.ds(0, rows_all - 1)], send_sems.at[9])
    drain(kn_recv.at[pl.ds(0, n_col - 1)], send_sems.at[10])
    drain(p7_recv.at[pl.ds(0, group - 1)], send_sems.at[11])
    drain(p8_recv.at[pl.ds(0, group - 1)], send_sems.at[12])


def fused(
    rhs_root, rhs_child, subtree_update, inv_root, inv_child, off_child, child_map, subtree_map
):
    n_col = lax.axis_size("col")
    n_row = lax.axis_size("row")
    n_leaf = lax.axis_size("leaf")
    panel = rhs_child.shape[0]
    right = panel * n_col
    sep = rhs_child.shape[2]
    ranks = n_row * (n_leaf // 2)
    rows_all = n_leaf * n_row
    group = ranks * n_col
    everyone = rows_all * n_col
    root_width = inv_root.shape[2]
    child_width = inv_child.shape[2]
    sep_blocks = child_width * n_col // BLOCK_ROWS
    root_blocks = root_width * n_col // BLOCK_ROWS
    sub_count = subtree_map.shape[1]
    upd_count = child_map.shape[1]

    number = jnp.arange(sub_count, dtype=jnp.int32)
    half = (jnp.arange(4, dtype=jnp.int32) % 2)[:, None]
    within = (number % n_row) * n_col + number // n_row
    sub_table = inverse_table(subtree_map, sep_blocks + upd_count, within)
    sub_table = jnp.where(sub_table >= 0, sub_table + half * n_row * n_col, -1)
    number = jnp.arange(upd_count, dtype=jnp.int32)
    root_table = inverse_table(child_map, root_blocks, (number % ranks) * n_col + number // ranks)
    child = jnp.arange(2, dtype=jnp.int32)[:, None]
    root_table = jnp.where(root_table >= 0, root_table + child * ranks * n_col, -1)
    beyond = jnp.clip(subtree_map - sep_blocks, 0)
    known = jnp.take_along_axis(jnp.repeat(child_map, 2, axis=0), beyond, axis=1)
    leaf_table = jnp.where(subtree_map < sep_blocks, subtree_map, sep_blocks + known)

    def turn(array):
        return array.transpose(1, 0, 2)

    smem = pl.BlockSpec(memory_space=pltpu.SMEM)
    vmem = pl.BlockSpec(memory_space=pltpu.VMEM)
    hbm = pl.BlockSpec(memory_space=pl.ANY)
    buffer = lambda *shape: pltpu.VMEM(shape, BF16)
    outs = pl.pallas_call(
        functools.partial(solve_kernel, (n_leaf, n_row, n_col)),
        out_shape=(
            jax.ShapeDtypeStruct((n_col, panel, sep), F32),
            jax.ShapeDtypeStruct((n_col, panel, sep), F32),
            jax.ShapeDtypeStruct((n_col, panel, BLOCK_ROWS), BF16),
        ),
        in_specs=[smem] * 4 + [vmem] * 3 + [hbm] * 3,
        out_specs=(vmem, vmem, vmem),
        scratch_shapes=[
            buffer(*inv_root.shape), buffer(*inv_child.shape), buffer(*off_child.shape),
            buffer(group * n_col, panel, BLOCK_ROWS),
            buffer(group, panel, sep),
            buffer(rows_all, n_col, panel, sep),
            buffer(n_col, right, sep), buffer(group, right, sep),
            buffer(n_col, n_col, panel, BLOCK_ROWS), buffer(n_col, n_col, panel, BLOCK_ROWS),
            buffer(n_col, panel, BLOCK_ROWS), buffer(rows_all * n_col, panel, BLOCK_ROWS),
            buffer(n_col, panel, root_width), buffer(n_col, panel, root_width),
            buffer(n_col, right, sep), buffer(n_col, n_col, right, sep),
            buffer(everyone, panel, sep), buffer(everyone, panel, sep),
            buffer(n_col, panel, sep), buffer(rows_all, n_col, panel, sep),
            buffer(n_col, panel, BLOCK_ROWS), buffer(n_col, n_col, panel, BLOCK_ROWS),
            buffer(ranks, right, sep), buffer(group, right, sep),
            buffer(n_col, panel, child_width), buffer(group, panel, child_width),
            buffer(sep_blocks + root_blocks, panel, BLOCK_ROWS),
            pltpu.VMEM((n_col, ranks, panel, sep), F32),
            pltpu.SemaphoreType.DMA((3,)),
            pltpu.SemaphoreType.DMA((13,)),
            pltpu.SemaphoreType.DMA((13,)),
        ],
        compiler_params=pltpu.CompilerParams(
            collective_id=0, has_side_effects=True, vmem_limit_bytes=32 * 1024 * 1024
        ),
    )(
        sub_table, root_table, leaf_table, child_map,
        turn(subtree_update), turn(rhs_child), turn(rhs_root), inv_root, inv_child, off_child,
    )
    return tuple(turn(out) for out in outs)


def body(*arrays):
    whole_blocks = (
        lax.axis_size("leaf") == 4
        and arrays[2].shape[2] == BLOCK_ROWS
        and arrays[4].shape[2] % BLOCK_ROWS == 0
        and arrays[0].shape[0] % 16 == 0
        and arrays[0].shape[2] % 16 == 0
    )
    return (fused if whole_blocks else local)(*arrays)


def solution(mesh):
    in_specs = (
        P("col", None, ("leaf", "row")),
        P("col", None, ("leaf", "row")),
        P("col", None, ("leaf", "row")),
        P(None, ("leaf", "row"), "col"),
        P(None, ("leaf", "row"), "col"),
        P(None, ("leaf", "row"), "col"),
        P(),
        P(),
    )
    out_specs = (
        P("col", None, ("leaf", "row")),
        P("col", None, ("leaf", "row")),
        P("col", None, ("leaf", "row")),
    )
    return jax.shard_map(body, mesh=mesh, in_specs=in_specs, out_specs=out_specs, check_vma=False)
```

```python
import functools

import jax
import jax.numpy as jnp
from jax import lax
from jax.experimental import pallas as pl
from jax.experimental.pallas import tpu as pltpu
from jax.sharding import PartitionSpec as P

BLOCK_ROWS = 128


def partner_2(block, axis, bit):
    count = lax.axis_size(axis)
    route = []
    for low in range(count):
        high = low | 1 << bit
        if high != low and high < count:
            route += [(low, high), (high, low)]
    return lax.ppermute(block, axis, route)


def group_gather(piece, group_size):
    merged = lax.all_gather(piece, "row", axis=2, tiled=True)
    leaf_index = lax.axis_index("leaf")
    for bit_number in range(group_size.bit_length() - 1):
        partner = partner_2(merged, "leaf", bit_number)
        upper = leaf_index >> bit_number & 1 == 1
        merged = jnp.where(
            upper, jnp.concatenate([partner, merged], 2), jnp.concatenate([merged, partner], 2)
        )
    return merged


def group_sum(partial_sum, group_size):
    leaf_index = lax.axis_index("leaf")
    for bit_number in reversed(range(group_size.bit_length() - 1)):
        middle = partial_sum.shape[1] // 2
        lower_half = partial_sum[:, :middle]
        upper_half = partial_sum[:, middle:]
        upper = leaf_index >> bit_number & 1 == 1
        outgoing = jnp.where(upper, lower_half, upper_half)
        kept_half = jnp.where(upper, upper_half, lower_half)
        partial_sum = kept_half + partner_2(
            outgoing.astype(jnp.bfloat16), "leaf", bit_number
        ).astype(outgoing.dtype)
    return lax.psum_scatter(
        partial_sum.astype(jnp.bfloat16), "row", scatter_dimension=1, tiled=True
    ).astype(jnp.float32)


def one_hot(block_map, blocks_total):
    return (block_map[..., None] == jnp.arange(blocks_total, dtype=jnp.int32)).astype(jnp.bfloat16)


def pick_piece(source, position, along):
    return lax.dynamic_index_in_dim(source, position, along, keepdims=False)


def contract(left_side, right_side, left_dim, right_dim):
    return lax.dot_general(
        left_side,
        right_side,
        (((left_dim,), (right_dim,)), ((), ())),
        preferred_element_type=jnp.float32,
    )


def local(
    rhs_root, rhs_child, subtree_update, inv_root, inv_child, off_child, child_map, subtree_map
):
    n_col = lax.axis_size("col")
    n_row = lax.axis_size("row")
    n_leaf = lax.axis_size("leaf")
    group_size = n_leaf // 2
    sub_size = n_leaf // 4
    col_index = lax.axis_index("col")
    leaf_index = lax.axis_index("leaf")
    row_index = lax.axis_index("row")
    front_index = leaf_index // group_size
    member = leaf_index % group_size
    child_rank = member * n_row + row_index
    half_index = member // sub_size
    sub_rank = member % sub_size * n_row + row_index
    panel_width = rhs_child.shape[0]
    right_sides = panel_width * n_col
    sep_piece = rhs_child.shape[2]
    upd_piece = subtree_update.shape[2]
    root_width = inv_root.shape[2]
    child_width = inv_child.shape[2]
    child_order = child_width * n_col
    child_update = upd_piece * n_col * group_size * n_row
    root_blocks = root_width * n_col // BLOCK_ROWS
    child_blocks = (child_order + child_update) // BLOCK_ROWS
    root_matrix = inv_root.reshape(n_col * sep_piece, root_width)
    child_matrix = inv_child.reshape(n_col * sep_piece, child_width)
    off_matrix = off_child.reshape(n_col * upd_piece, child_width)
    joined = jnp.concatenate([subtree_update, rhs_child], 2)
    gathered = group_gather(joined, group_size).reshape(
        panel_width, n_col, group_size * n_row, upd_piece + sep_piece
    )
    sub_vectors = (
        gathered[..., :upd_piece]
        .reshape(panel_width, n_col, 2, -1)
        .transpose(2, 0, 1, 3)
        .reshape(2, panel_width, -1, BLOCK_ROWS)
    )
    child_rhs_full = gathered[..., upd_piece:].reshape(panel_width, child_order)
    sub_rows = lax.dynamic_slice_in_dim(subtree_map, 2 * front_index, 2, 0)
    spread = jnp.einsum(
        "hpjt,hjn->pnt",
        sub_vectors,
        one_hot(sub_rows, child_blocks),
        preferred_element_type=jnp.float32,
    ).reshape(panel_width, -1)
    child_sep = (spread[:, :child_order] + child_rhs_full.astype(jnp.float32)).astype(jnp.bfloat16)
    child_tail = spread[:, child_order:]
    child_tile = lax.all_to_all(
        child_sep.reshape(panel_width, n_col, child_width),
        "col",
        split_axis=1,
        concat_axis=0,
        tiled=True,
    ).reshape(right_sides, child_width)
    child_forward = lax.psum(contract(child_tile, child_matrix, 1, 1), "col").astype(jnp.bfloat16)
    forward_quarter = lax.dynamic_slice_in_dim(
        child_forward.reshape(right_sides, n_col, sep_piece), col_index, 1, 1
    )
    forward_tile = group_gather(forward_quarter, group_size).reshape(right_sides, child_width)
    pass_term = lax.psum_scatter(
        contract(forward_tile, off_matrix, 1, 1), "col", scatter_dimension=0, tiled=True
    )
    tail_mine = pick_piece(
        child_tail.reshape(panel_width, n_col, group_size * n_row, upd_piece), child_rank, 2
    )
    child_pass = (tail_mine - pass_term.reshape(panel_width, n_col, upd_piece)).astype(jnp.bfloat16)
    joined_root = jnp.concatenate([child_pass, rhs_root], 2)
    root_all = lax.all_gather(joined_root, ("leaf", "row"), axis=2, tiled=True).reshape(
        panel_width, n_col, n_leaf * n_row, upd_piece + sep_piece
    )
    pass_vectors = (
        root_all[..., :upd_piece]
        .reshape(panel_width, n_col, 2, -1)
        .transpose(2, 0, 1, 3)
        .reshape(2, panel_width, -1, BLOCK_ROWS)
    )
    root_rhs_full = root_all[..., upd_piece:].reshape(panel_width, root_width * n_col)
    root_spread = jnp.einsum(
        "hpjt,hjn->pnt",
        pass_vectors,
        one_hot(child_map, root_blocks),
        preferred_element_type=jnp.float32,
    ).reshape(panel_width, -1)
    root_sep = (root_spread + root_rhs_full.astype(jnp.float32)).astype(jnp.bfloat16)
    root_tile = lax.all_to_all(
        root_sep.reshape(panel_width, n_col, root_width),
        "col",
        split_axis=1,
        concat_axis=0,
        tiled=True,
    ).reshape(right_sides, root_width)
    root_forward = lax.psum(contract(root_tile, root_matrix, 1, 1), "col").astype(jnp.bfloat16)
    map_row = pick_piece(child_map, front_index, 0)
    root_piece = lax.psum_scatter(
        contract(root_matrix, root_forward, 0, 1), ("leaf", "row"), scatter_dimension=0, tiled=True
    )
    solution_root = lax.all_to_all(
        root_piece.T.reshape(right_sides, 1, sep_piece),
        "col",
        split_axis=0,
        concat_axis=1,
        tiled=True,
    )
    root_everywhere = lax.all_gather(
        solution_root.astype(jnp.bfloat16), ("leaf", "row"), axis=2, tiled=True
    ).reshape(panel_width, root_blocks, BLOCK_ROWS)
    known_full = (
        jnp.einsum(
            "pnt,jn->pjt",
            root_everywhere,
            one_hot(map_row, root_blocks),
            preferred_element_type=jnp.float32,
        )
        .astype(jnp.bfloat16)
        .reshape(panel_width, child_update)
    )
    known_mine = pick_piece(
        known_full.reshape(panel_width, n_col, group_size * n_row, upd_piece), child_rank, 2
    )
    known_rows = lax.all_gather(known_mine, "col", axis=0, tiled=True).reshape(
        right_sides, n_col * upd_piece
    )
    correction = group_sum(contract(known_rows, off_matrix, 1, 0), group_size)
    back_quarter = (
        forward_quarter.reshape(right_sides, sep_piece).astype(jnp.float32) - correction
    ).astype(jnp.bfloat16)
    back_rows = lax.all_gather(
        back_quarter.reshape(right_sides, 1, sep_piece), "col", axis=1, tiled=True
    ).reshape(right_sides, n_col * sep_piece)
    child_piece = group_sum(contract(back_rows, child_matrix, 1, 0), group_size)
    solution_child = lax.all_to_all(
        child_piece.reshape(right_sides, 1, sep_piece),
        "col",
        split_axis=0,
        concat_axis=1,
        tiled=True,
    )
    child_rounded = solution_child.astype(jnp.bfloat16)
    sep_whole = group_gather(child_rounded, group_size).reshape(panel_width, child_order)
    child_whole = jnp.concatenate([sep_whole, known_full], 1)
    sub_row = pick_piece(subtree_map, 2 * front_index + half_index, 0)
    leaf_full = jnp.einsum(
        "pnt,jn->pjt",
        child_whole.reshape(panel_width, child_blocks, BLOCK_ROWS),
        one_hot(sub_row, child_blocks),
        preferred_element_type=jnp.float32,
    ).astype(jnp.bfloat16)
    leaf_solution = pick_piece(
        leaf_full.reshape(panel_width, n_col, sub_size * n_row, upd_piece), sub_rank, 2
    )
    return (solution_root, solution_child, leaf_solution)


F32 = jnp.float32
BF16 = jnp.bfloat16


def inverse_table(block_map, blocks_total, places):
    hit = block_map[..., None] == jnp.arange(blocks_total, dtype=jnp.int32)
    return jnp.sum(jnp.where(hit, places[:, None] + 1, 0), axis=-2, dtype=jnp.int32) - 1


def add_up(terms):
    total = terms[0]
    for term in terms[1:]:
        total = total + term
    return total


def solve_kernel(
    dims,
    sub_table, root_table, leaf_table, child_map,
    sub_in, rc_in, rr_in, root_hbm, child_hbm, off_hbm,
    root_out, child_out, leaf_out,
    root_w, child_w, off_w,
    sub_buf, rc_buf, rr_buf,
    p2_send, p2_recv, p3_send, p3_recv, pass_send, pass_buf,
    fw_send, fw_recv, p5_send, p5_recv,
    sr_send, sr_recv, p7_send, p7_recv, p8_send, p8_recv,
    blocks, pieces,
    load_sems, send_sems, recv_sems, share_sems, shared_sems,
):
    n_leaf, n_row, n_col = dims
    panel = sub_in.shape[1]
    sep = rc_in.shape[2]
    ranks = n_row * (n_leaf // 2)
    rows_all = n_leaf * n_row
    group = ranks * n_col
    right = panel * n_col
    child_tile_blocks = child_w.shape[3] // BLOCK_ROWS
    root_tile_blocks = root_w.shape[3] // BLOCK_ROWS
    sep_blocks = child_tile_blocks * n_col
    c = lax.axis_index("col")
    leaf = lax.axis_index("leaf")
    row = lax.axis_index("row")
    half = n_leaf // 2
    front = lax.div(leaf, half)
    rank = lax.rem(leaf, half) * n_row + row
    r = leaf * n_row + row
    gid = c * ranks + rank

    loads = [
        pltpu.make_async_copy(child_hbm, child_w.at[c], load_sems.at[0]),
        pltpu.make_async_copy(off_hbm, off_w.at[c], load_sems.at[1]),
        pltpu.make_async_copy(root_hbm, root_w.at[c], load_sems.at[2]),
    ]
    for load in loads:
        load.start()

    def at_row(r2, c2):
        return {"leaf": lax.div(r2, n_row), "row": lax.rem(r2, n_row), "col": c2}

    def at_group(g2):
        return at_row(front * ranks + lax.rem(g2, ranks), lax.div(g2, ranks))

    def each(count, own, body):
        def step(k, carry):
            body(lax.rem(own + k, count))
            return carry

        lax.fori_loop(1, count, step, 0)

    def push(source, target, phase, device):
        pltpu.make_async_remote_copy(
            src_ref=source,
            dst_ref=target,
            send_sem=send_sems.at[phase],
            recv_sem=recv_sems.at[phase],
            device_id=device,
            device_id_type=pl.DeviceIdType.MESH,
        ).start()

    def drain(view, sem):
        pltpu.make_async_copy(view, view, sem).wait()

    barrier = pltpu.get_barrier_semaphore()

    def greet(device):
        pl.semaphore_signal(
            barrier, inc=1, device_id=device, device_id_type=pl.DeviceIdType.MESH
        )

    pair = c + 1 - 2 * lax.rem(c, 2)
    across = lax.rem(c + 2, n_col)

    def hand(weights, slot, number, kind, c2):
        pltpu.make_async_remote_copy(
            src_ref=weights.at[slot],
            dst_ref=weights.at[slot],
            send_sem=share_sems.at[number, kind],
            recv_sem=shared_sems.at[number, kind],
            device_id=at_row(r, c2),
            device_id_type=pl.DeviceIdType.MESH,
        ).start()

    def share(weights, number):
        hand(weights, c, number, 0, across)
        hand(weights, c, number, 1, pair)

    def relay(weights, number):
        drain(weights.at[across], shared_sems.at[number, 0])
        hand(weights, across, number, 2, pair)

    def settle(weights, number):
        drain(weights.at[0], shared_sems.at[number, 1])
        drain(weights.at[0], shared_sems.at[number, 2])

    def flat(weights, c2):
        return weights[c2].reshape(-1, weights.shape[3])

    each(group, gid, lambda g2: greet(at_group(g2)))
    for k in range(ranks):
        greet(at_row((1 - front) * ranks + k, c))
    pl.semaphore_wait(barrier, group - 1 + ranks)

    each(group, gid, lambda g2: push(rc_in.at[lax.div(g2, ranks)], rc_buf.at[gid], 1, at_group(g2)))
    each(group, gid, lambda g2: push(sub_in, sub_buf.at[pl.ds(gid * n_col, n_col)], 0, at_group(g2)))
    each(rows_all, r, lambda r2: push(rr_in, rr_buf.at[r], 2, at_row(r2, c)))
    sub_buf[pl.ds(gid * n_col, n_col)] = sub_in[...]
    rc_buf[gid] = rc_in[c]
    rr_buf[r] = rr_in[...]
    loads[2].wait()
    share(root_w, 2)
    loads[0].wait()
    drain(rc_buf.at[pl.ds(0, group - 1)], recv_sems.at[1])
    drain(sub_buf.at[pl.ds(0, (group - 1) * n_col)], recv_sems.at[0])

    def placed(p, block):
        total = None
        for h in range(2):
            place = sub_table[2 * front + h, block]
            value = sub_buf[p * ranks * n_col + jnp.maximum(place, 0)].astype(F32)
            value = jnp.where(place >= 0, value, jnp.zeros_like(value))
            total = value if total is None else total + value
        return total

    def rows_of(values):
        return jnp.concatenate(values, 0)

    x = jnp.concatenate(
        [rows_of([rc_buf[p * ranks + k] for p in range(n_col)]).astype(F32) for k in range(ranks)], 1
    )
    x = x + jnp.concatenate(
        [
            rows_of([placed(p, c * child_tile_blocks + b) for p in range(n_col)])
            for b in range(child_tile_blocks)
        ],
        1,
    )
    x = x.astype(BF16)
    for q in range(n_col):
        p2_send[q] = contract(x, child_w[c, q], 1, 1).astype(BF16)

    each(group, gid, lambda g2: push(p2_send.at[lax.div(g2, ranks)], p2_recv.at[gid], 3, at_group(g2)))
    p2_recv[gid] = p2_send[c]
    tail = [placed(c, sep_blocks + q * ranks + rank) for q in range(n_col)]
    loads[1].wait()
    drain(p2_recv.at[pl.ds(0, group - 1)], recv_sems.at[3])
    forward = [
        add_up([p2_recv[c2 * ranks + k].astype(F32) for c2 in range(n_col)]).astype(BF16)
        for k in range(ranks)
    ]
    y = jnp.concatenate([piece.astype(F32) for piece in forward], 1).astype(BF16)
    for q in range(n_col):
        z = contract(y, off_w[c, q], 1, 1).astype(BF16)
        for p in range(n_col):
            p3_send[p, q] = z[p * panel : (p + 1) * panel]

    each(n_col, c, lambda c2: push(p3_send.at[c2], p3_recv.at[c], 4, at_row(r, c2)))
    p3_recv[c] = p3_send[c]
    own = add_up([p2_recv[c2 * ranks + rank].astype(F32) for c2 in range(n_col)])
    fw_send[...] = own.astype(BF16).reshape(fw_send.shape)
    each(n_col, c, lambda c2: push(fw_send.at[c2], fw_recv.at[c], 6, at_row(r, c2)))
    fw_recv[c] = fw_send[c]
    share(off_w, 1)
    drain(p3_recv.at[pl.ds(0, n_col - 1)], recv_sems.at[4])
    for q in range(n_col):
        total = add_up([p3_recv[c2, q].astype(F32) for c2 in range(n_col)])
        pass_send[q] = (tail[q] - total).astype(BF16)

    each(rows_all, r, lambda r2: push(pass_send, pass_buf.at[pl.ds(r * n_col, n_col)], 5, at_row(r2, c)))
    pass_buf[pl.ds(r * n_col, n_col)] = pass_send[...]
    relay(root_w, 2)
    drain(rr_buf.at[pl.ds(0, rows_all - 1)], recv_sems.at[2])
    x = jnp.concatenate(
        [rr_buf[k].reshape(right, sep).astype(F32) for k in range(rows_all)], 1
    )
    drain(pass_buf.at[pl.ds(0, (rows_all - 1) * n_col)], recv_sems.at[5])

    def passed(block):
        total = None
        for f in range(2):
            place = root_table[f, block]
            value = pass_buf[jnp.maximum(place, 0)].astype(F32)
            value = jnp.where(place >= 0, value, jnp.zeros_like(value))
            total = value if total is None else total + value
        return total

    x = x + jnp.concatenate(
        [
            rows_of([passed(q * root_tile_blocks + b) for q in range(n_col)])
            for b in range(root_tile_blocks)
        ],
        1,
    )
    x = x.astype(BF16)
    settle(root_w, 2)
    root_forward = add_up(
        [
            contract(x[c2 * panel : (c2 + 1) * panel], flat(root_w, c2), 1, 1)
            for c2 in range(n_col)
        ]
    ).astype(BF16)
    for c2 in range(n_col):
        total = contract(root_forward, flat(root_w, c2), 1, 0)
        for r2 in range(rows_all):
            p5_send[r2, c2] = total[:, r2 * sep : (r2 + 1) * sep].astype(BF16)

    each(rows_all, r, lambda r2: push(p5_send.at[r2], p5_recv.at[r], 7, at_row(r2, c)))
    p5_recv[r] = p5_send[r]
    share(child_w, 0)
    drain(p5_recv.at[pl.ds(0, rows_all - 1)], recv_sems.at[7])
    for q in range(n_col):
        total = add_up([p5_recv[k, q].astype(F32) for k in range(rows_all)])
        root_out[q] = total
        sr_send[q] = total.astype(BF16)

    each(rows_all, r, lambda r2: push(sr_send, sr_recv.at[r], 8, at_row(r2, c)))
    sr_recv[r] = sr_send[...]
    relay(off_w, 1)
    drain(sr_recv.at[pl.ds(0, rows_all - 1)], recv_sems.at[8])
    x = jnp.concatenate(
        [sr_recv[k].reshape(right, sep).astype(F32) for k in range(rows_all)], 1
    ).astype(BF16)
    for q in range(n_col):
        for b in range(root_tile_blocks):
            blocks[sep_blocks + q * root_tile_blocks + b] = x[
                q * panel : (q + 1) * panel, b * BLOCK_ROWS : (b + 1) * BLOCK_ROWS
            ]
    known = jnp.concatenate(
        [blocks[sep_blocks + child_map[front, q * ranks + rank]] for q in range(n_col)], 1
    )
    settle(off_w, 1)
    for c2 in range(n_col):
        total = contract(known, flat(off_w, c2), 1, 0)
        for k in range(ranks):
            p7_send[k, c2] = total[:, k * sep : (k + 1) * sep].astype(BF16)

    def each_rank(body):
        each(ranks, rank, lambda k: body(k, at_row(front * ranks + k, c)))

    each_rank(lambda k, device: push(p7_send.at[k], p7_recv.at[rank], 9, device))
    p7_recv[rank] = p7_send[rank]
    relay(child_w, 0)
    drain(fw_recv.at[pl.ds(0, n_col - 1)], recv_sems.at[6])
    drain(p7_recv.at[pl.ds(0, ranks - 1)], recv_sems.at[9])
    back = []
    for q in range(n_col):
        total = add_up([p7_recv[k, q].astype(F32) for k in range(ranks)])
        back.append(fw_recv[q].astype(F32) - total)
    back = jnp.concatenate(back, 1).astype(BF16)
    settle(child_w, 0)
    for c2 in range(n_col):
        p8_send[c2] = contract(back, flat(child_w, c2), 1, 0).astype(BF16)

    each_rank(lambda k, device: push(p8_send, p8_recv.at[rank], 10, device))
    p8_recv[rank] = p8_send[...]
    drain(p8_recv.at[pl.ds(0, ranks - 1)], recv_sems.at[10])
    for q in range(n_col):
        total = add_up([p8_recv[k, q].astype(F32) for k in range(ranks)])
        for k in range(ranks):
            pieces[q, k] = total[:, k * sep : (k + 1) * sep]
        child_out[q] = pieces[q, rank]
        total = total.astype(BF16)
        for b in range(child_tile_blocks):
            blocks[q * child_tile_blocks + b] = total[:, b * BLOCK_ROWS : (b + 1) * BLOCK_ROWS]
    for q in range(n_col):
        leaf_out[q] = blocks[leaf_table[leaf, q * n_row + row]]

    drain(rc_buf.at[pl.ds(0, group - 1)], send_sems.at[1])
    drain(sub_buf.at[pl.ds(0, (group - 1) * n_col)], send_sems.at[0])
    drain(rr_buf.at[pl.ds(0, rows_all - 1)], send_sems.at[2])
    drain(p2_recv.at[pl.ds(0, group - 1)], send_sems.at[3])
    drain(p3_recv.at[pl.ds(0, n_col - 1)], send_sems.at[4])
    drain(pass_buf.at[pl.ds(0, (rows_all - 1) * n_col)], send_sems.at[5])
    drain(fw_recv.at[pl.ds(0, n_col - 1)], send_sems.at[6])
    drain(p5_recv.at[pl.ds(0, rows_all - 1)], send_sems.at[7])
    drain(sr_recv.at[pl.ds(0, rows_all - 1)], send_sems.at[8])
    drain(p7_recv.at[pl.ds(0, ranks - 1)], send_sems.at[9])
    drain(p8_recv.at[pl.ds(0, ranks - 1)], send_sems.at[10])
    for number, weights in enumerate((child_w, off_w, root_w)):
        for kind in range(3):
            drain(weights.at[0], share_sems.at[number, kind])


def fused(
    rhs_root, rhs_child, subtree_update, inv_root, inv_child, off_child, child_map, subtree_map
):
    n_col = lax.axis_size("col")
    n_row = lax.axis_size("row")
    n_leaf = lax.axis_size("leaf")
    panel = rhs_child.shape[0]
    right = panel * n_col
    sep = rhs_child.shape[2]
    ranks = n_row * (n_leaf // 2)
    rows_all = n_leaf * n_row
    group = ranks * n_col
    root_width = inv_root.shape[2]
    child_width = inv_child.shape[2]
    sep_blocks = child_width * n_col // BLOCK_ROWS
    root_blocks = root_width * n_col // BLOCK_ROWS
    sub_count = subtree_map.shape[1]
    upd_count = child_map.shape[1]

    number = jnp.arange(sub_count, dtype=jnp.int32)
    half = (jnp.arange(4, dtype=jnp.int32) % 2)[:, None]
    within = (number % n_row) * n_col + number // n_row
    sub_table = inverse_table(subtree_map, sep_blocks + upd_count, within)
    sub_table = jnp.where(sub_table >= 0, sub_table + half * n_row * n_col, -1)
    number = jnp.arange(upd_count, dtype=jnp.int32)
    root_table = inverse_table(child_map, root_blocks, (number % ranks) * n_col + number // ranks)
    child = jnp.arange(2, dtype=jnp.int32)[:, None]
    root_table = jnp.where(root_table >= 0, root_table + child * ranks * n_col, -1)
    beyond = jnp.clip(subtree_map - sep_blocks, 0)
    known = jnp.take_along_axis(jnp.repeat(child_map, 2, axis=0), beyond, axis=1)
    leaf_table = jnp.where(subtree_map < sep_blocks, subtree_map, sep_blocks + known)

    def turn(array):
        return array.transpose(1, 0, 2)

    smem = pl.BlockSpec(memory_space=pltpu.SMEM)
    vmem = pl.BlockSpec(memory_space=pltpu.VMEM)
    hbm = pl.BlockSpec(memory_space=pl.ANY)
    buffer = lambda *shape: pltpu.VMEM(shape, BF16)
    outs = pl.pallas_call(
        functools.partial(solve_kernel, (n_leaf, n_row, n_col)),
        out_shape=(
            jax.ShapeDtypeStruct((n_col, panel, sep), F32),
            jax.ShapeDtypeStruct((n_col, panel, sep), F32),
            jax.ShapeDtypeStruct((n_col, panel, BLOCK_ROWS), BF16),
        ),
        in_specs=[smem] * 4 + [vmem] * 3 + [hbm] * 3,
        out_specs=(vmem, vmem, vmem),
        scratch_shapes=[
            buffer(n_col, *inv_root.shape), buffer(n_col, *inv_child.shape),
            buffer(n_col, *off_child.shape),
            buffer(group * n_col, panel, BLOCK_ROWS),
            buffer(group, panel, sep),
            buffer(rows_all, n_col, panel, sep),
            buffer(n_col, right, sep), buffer(group, right, sep),
            buffer(n_col, n_col, panel, BLOCK_ROWS), buffer(n_col, n_col, panel, BLOCK_ROWS),
            buffer(n_col, panel, BLOCK_ROWS), buffer(rows_all * n_col, panel, BLOCK_ROWS),
            buffer(n_col, panel, sep), buffer(n_col, panel, sep),
            buffer(rows_all, n_col, panel, sep), buffer(rows_all, n_col, panel, sep),
            buffer(n_col, panel, sep), buffer(rows_all, n_col, panel, sep),
            buffer(ranks, n_col, panel, sep), buffer(ranks, n_col, panel, sep),
            buffer(n_col, panel, child_width), buffer(ranks, n_col, panel, child_width),
            buffer(sep_blocks + root_blocks, panel, BLOCK_ROWS),
            pltpu.VMEM((n_col, ranks, panel, sep), F32),
            pltpu.SemaphoreType.DMA((3,)),
            pltpu.SemaphoreType.DMA((11,)),
            pltpu.SemaphoreType.DMA((11,)),
            pltpu.SemaphoreType.DMA((3, 3)),
            pltpu.SemaphoreType.DMA((3, 3)),
        ],
        compiler_params=pltpu.CompilerParams(
            collective_id=0, has_side_effects=True, vmem_limit_bytes=32 * 1024 * 1024
        ),
    )(
        sub_table, root_table, leaf_table, child_map,
        turn(subtree_update), turn(rhs_child), turn(rhs_root), inv_root, inv_child, off_child,
    )
    return tuple(turn(out) for out in outs)


def body(*arrays):
    whole_blocks = (
        lax.axis_size("leaf") == 4
        and arrays[2].shape[2] == BLOCK_ROWS
        and arrays[4].shape[2] % BLOCK_ROWS == 0
        and arrays[0].shape[0] % 16 == 0
        and arrays[0].shape[2] % 16 == 0
    )
    return (fused if whole_blocks else local)(*arrays)


def solution(mesh):
    in_specs = (
        P("col", None, ("leaf", "row")),
        P("col", None, ("leaf", "row")),
        P("col", None, ("leaf", "row")),
        P(None, ("leaf", "row"), "col"),
        P(None, ("leaf", "row"), "col"),
        P(None, ("leaf", "row"), "col"),
        P(),
        P(),
    )
    out_specs = (
        P("col", None, ("leaf", "row")),
        P("col", None, ("leaf", "row")),
        P("col", None, ("leaf", "row")),
    )
    return jax.shard_map(body, mesh=mesh, in_specs=in_specs, out_specs=out_specs, check_vma=False)
```

```python
import functools

import jax
import jax.numpy as jnp
from jax import lax
from jax.experimental import pallas as pl
from jax.experimental.pallas import tpu as pltpu
from jax.sharding import PartitionSpec as P

BLOCK_ROWS = 128


def partner_2(block, axis, bit):
    count = lax.axis_size(axis)
    route = []
    for low in range(count):
        high = low | 1 << bit
        if high != low and high < count:
            route += [(low, high), (high, low)]
    return lax.ppermute(block, axis, route)


def group_gather(piece, group_size):
    merged = lax.all_gather(piece, "row", axis=2, tiled=True)
    leaf_index = lax.axis_index("leaf")
    for bit_number in range(group_size.bit_length() - 1):
        partner = partner_2(merged, "leaf", bit_number)
        upper = leaf_index >> bit_number & 1 == 1
        merged = jnp.where(
            upper, jnp.concatenate([partner, merged], 2), jnp.concatenate([merged, partner], 2)
        )
    return merged


def group_sum(partial_sum, group_size):
    leaf_index = lax.axis_index("leaf")
    for bit_number in reversed(range(group_size.bit_length() - 1)):
        middle = partial_sum.shape[1] // 2
        lower_half = partial_sum[:, :middle]
        upper_half = partial_sum[:, middle:]
        upper = leaf_index >> bit_number & 1 == 1
        outgoing = jnp.where(upper, lower_half, upper_half)
        kept_half = jnp.where(upper, upper_half, lower_half)
        partial_sum = kept_half + partner_2(
            outgoing.astype(jnp.bfloat16), "leaf", bit_number
        ).astype(outgoing.dtype)
    return lax.psum_scatter(
        partial_sum.astype(jnp.bfloat16), "row", scatter_dimension=1, tiled=True
    ).astype(jnp.float32)


def one_hot(block_map, blocks_total):
    return (block_map[..., None] == jnp.arange(blocks_total, dtype=jnp.int32)).astype(jnp.bfloat16)


def pick_piece(source, position, along):
    return lax.dynamic_index_in_dim(source, position, along, keepdims=False)


def contract(left_side, right_side, left_dim, right_dim):
    return lax.dot_general(
        left_side,
        right_side,
        (((left_dim,), (right_dim,)), ((), ())),
        preferred_element_type=jnp.float32,
    )


def local(
    rhs_root, rhs_child, subtree_update, inv_root, inv_child, off_child, child_map, subtree_map
):
    n_col = lax.axis_size("col")
    n_row = lax.axis_size("row")
    n_leaf = lax.axis_size("leaf")
    group_size = n_leaf // 2
    sub_size = n_leaf // 4
    col_index = lax.axis_index("col")
    leaf_index = lax.axis_index("leaf")
    row_index = lax.axis_index("row")
    front_index = leaf_index // group_size
    member = leaf_index % group_size
    child_rank = member * n_row + row_index
    half_index = member // sub_size
    sub_rank = member % sub_size * n_row + row_index
    panel_width = rhs_child.shape[0]
    right_sides = panel_width * n_col
    sep_piece = rhs_child.shape[2]
    upd_piece = subtree_update.shape[2]
    root_width = inv_root.shape[2]
    child_width = inv_child.shape[2]
    child_order = child_width * n_col
    child_update = upd_piece * n_col * group_size * n_row
    root_blocks = root_width * n_col // BLOCK_ROWS
    child_blocks = (child_order + child_update) // BLOCK_ROWS
    root_matrix = inv_root.reshape(n_col * sep_piece, root_width)
    child_matrix = inv_child.reshape(n_col * sep_piece, child_width)
    off_matrix = off_child.reshape(n_col * upd_piece, child_width)
    joined = jnp.concatenate([subtree_update, rhs_child], 2)
    gathered = group_gather(joined, group_size).reshape(
        panel_width, n_col, group_size * n_row, upd_piece + sep_piece
    )
    sub_vectors = (
        gathered[..., :upd_piece]
        .reshape(panel_width, n_col, 2, -1)
        .transpose(2, 0, 1, 3)
        .reshape(2, panel_width, -1, BLOCK_ROWS)
    )
    child_rhs_full = gathered[..., upd_piece:].reshape(panel_width, child_order)
    sub_rows = lax.dynamic_slice_in_dim(subtree_map, 2 * front_index, 2, 0)
    spread = jnp.einsum(
        "hpjt,hjn->pnt",
        sub_vectors,
        one_hot(sub_rows, child_blocks),
        preferred_element_type=jnp.float32,
    ).reshape(panel_width, -1)
    child_sep = (spread[:, :child_order] + child_rhs_full.astype(jnp.float32)).astype(jnp.bfloat16)
    child_tail = spread[:, child_order:]
    child_tile = lax.all_to_all(
        child_sep.reshape(panel_width, n_col, child_width),
        "col",
        split_axis=1,
        concat_axis=0,
        tiled=True,
    ).reshape(right_sides, child_width)
    child_forward = lax.psum(contract(child_tile, child_matrix, 1, 1), "col").astype(jnp.bfloat16)
    forward_quarter = lax.dynamic_slice_in_dim(
        child_forward.reshape(right_sides, n_col, sep_piece), col_index, 1, 1
    )
    forward_tile = group_gather(forward_quarter, group_size).reshape(right_sides, child_width)
    pass_term = lax.psum_scatter(
        contract(forward_tile, off_matrix, 1, 1), "col", scatter_dimension=0, tiled=True
    )
    tail_mine = pick_piece(
        child_tail.reshape(panel_width, n_col, group_size * n_row, upd_piece), child_rank, 2
    )
    child_pass = (tail_mine - pass_term.reshape(panel_width, n_col, upd_piece)).astype(jnp.bfloat16)
    joined_root = jnp.concatenate([child_pass, rhs_root], 2)
    root_all = lax.all_gather(joined_root, ("leaf", "row"), axis=2, tiled=True).reshape(
        panel_width, n_col, n_leaf * n_row, upd_piece + sep_piece
    )
    pass_vectors = (
        root_all[..., :upd_piece]
        .reshape(panel_width, n_col, 2, -1)
        .transpose(2, 0, 1, 3)
        .reshape(2, panel_width, -1, BLOCK_ROWS)
    )
    root_rhs_full = root_all[..., upd_piece:].reshape(panel_width, root_width * n_col)
    root_spread = jnp.einsum(
        "hpjt,hjn->pnt",
        pass_vectors,
        one_hot(child_map, root_blocks),
        preferred_element_type=jnp.float32,
    ).reshape(panel_width, -1)
    root_sep = (root_spread + root_rhs_full.astype(jnp.float32)).astype(jnp.bfloat16)
    root_tile = lax.all_to_all(
        root_sep.reshape(panel_width, n_col, root_width),
        "col",
        split_axis=1,
        concat_axis=0,
        tiled=True,
    ).reshape(right_sides, root_width)
    root_forward = lax.psum(contract(root_tile, root_matrix, 1, 1), "col").astype(jnp.bfloat16)
    map_row = pick_piece(child_map, front_index, 0)
    root_piece = lax.psum_scatter(
        contract(root_matrix, root_forward, 0, 1), ("leaf", "row"), scatter_dimension=0, tiled=True
    )
    solution_root = lax.all_to_all(
        root_piece.T.reshape(right_sides, 1, sep_piece),
        "col",
        split_axis=0,
        concat_axis=1,
        tiled=True,
    )
    root_everywhere = lax.all_gather(
        solution_root.astype(jnp.bfloat16), ("leaf", "row"), axis=2, tiled=True
    ).reshape(panel_width, root_blocks, BLOCK_ROWS)
    known_full = (
        jnp.einsum(
            "pnt,jn->pjt",
            root_everywhere,
            one_hot(map_row, root_blocks),
            preferred_element_type=jnp.float32,
        )
        .astype(jnp.bfloat16)
        .reshape(panel_width, child_update)
    )
    known_mine = pick_piece(
        known_full.reshape(panel_width, n_col, group_size * n_row, upd_piece), child_rank, 2
    )
    known_rows = lax.all_gather(known_mine, "col", axis=0, tiled=True).reshape(
        right_sides, n_col * upd_piece
    )
    correction = group_sum(contract(known_rows, off_matrix, 1, 0), group_size)
    back_quarter = (
        forward_quarter.reshape(right_sides, sep_piece).astype(jnp.float32) - correction
    ).astype(jnp.bfloat16)
    back_rows = lax.all_gather(
        back_quarter.reshape(right_sides, 1, sep_piece), "col", axis=1, tiled=True
    ).reshape(right_sides, n_col * sep_piece)
    child_piece = group_sum(contract(back_rows, child_matrix, 1, 0), group_size)
    solution_child = lax.all_to_all(
        child_piece.reshape(right_sides, 1, sep_piece),
        "col",
        split_axis=0,
        concat_axis=1,
        tiled=True,
    )
    child_rounded = solution_child.astype(jnp.bfloat16)
    sep_whole = group_gather(child_rounded, group_size).reshape(panel_width, child_order)
    child_whole = jnp.concatenate([sep_whole, known_full], 1)
    sub_row = pick_piece(subtree_map, 2 * front_index + half_index, 0)
    leaf_full = jnp.einsum(
        "pnt,jn->pjt",
        child_whole.reshape(panel_width, child_blocks, BLOCK_ROWS),
        one_hot(sub_row, child_blocks),
        preferred_element_type=jnp.float32,
    ).astype(jnp.bfloat16)
    leaf_solution = pick_piece(
        leaf_full.reshape(panel_width, n_col, sub_size * n_row, upd_piece), sub_rank, 2
    )
    return (solution_root, solution_child, leaf_solution)


F32 = jnp.float32
BF16 = jnp.bfloat16


def add_up(terms):
    total = terms[0]
    for term in terms[1:]:
        total = total + term
    return total


def solve_kernel(
    dims,
    child_map, subtree_map,
    sub_in, rc_in, rr_in, root_hbm, child_hbm, off_hbm,
    root_out, child_out, leaf_out,
    root_w, child_w, off_w,
    p1_send, p1_recv, tail_send, tail_recv, rr_buf,
    p2_send, p2_recv, p3_send, p3_recv, pass_send, pass_buf,
    fw_send, fw_recv, p5_send, p5_recv,
    sr_send, sr_recv, p7_send, p7_recv, p8_send, p8_recv,
    blocks, pieces,
    load_sems, send_sems, recv_sems, share_sems, shared_sems,
):
    n_leaf, n_row, n_col = dims
    panel = sub_in.shape[1]
    sep = rc_in.shape[2]
    ranks = n_row * (n_leaf // 2)
    rows_all = n_leaf * n_row
    group = ranks * n_col
    right = panel * n_col
    child_tile_blocks = child_w.shape[3] // BLOCK_ROWS
    root_tile_blocks = root_w.shape[3] // BLOCK_ROWS
    sep_blocks = child_tile_blocks * n_col
    c = lax.axis_index("col")
    leaf = lax.axis_index("leaf")
    row = lax.axis_index("row")
    half = n_leaf // 2
    front = lax.div(leaf, half)
    rank = lax.rem(leaf, half) * n_row + row
    r = leaf * n_row + row
    gid = c * ranks + rank

    loads = [
        pltpu.make_async_copy(child_hbm, child_w.at[c], load_sems.at[0]),
        pltpu.make_async_copy(off_hbm, off_w.at[c], load_sems.at[1]),
        pltpu.make_async_copy(root_hbm, root_w.at[c], load_sems.at[2]),
    ]
    for load in loads:
        load.start()

    def at_row(r2, c2):
        return {"leaf": lax.div(r2, n_row), "row": lax.rem(r2, n_row), "col": c2}

    def at_group(g2):
        return at_row(front * ranks + lax.rem(g2, ranks), lax.div(g2, ranks))

    def each(count, own, body):
        def step(k, carry):
            body(lax.rem(own + k, count))
            return carry

        lax.fori_loop(1, count, step, 0)

    def push(source, target, phase, device):
        pltpu.make_async_remote_copy(
            src_ref=source,
            dst_ref=target,
            send_sem=send_sems.at[phase],
            recv_sem=recv_sems.at[phase],
            device_id=device,
            device_id_type=pl.DeviceIdType.MESH,
        ).start()

    def drain(view, sem):
        pltpu.make_async_copy(view, view, sem).wait()

    barrier = pltpu.get_barrier_semaphore()

    def greet(device):
        pl.semaphore_signal(
            barrier, inc=1, device_id=device, device_id_type=pl.DeviceIdType.MESH
        )

    pair = c + 1 - 2 * lax.rem(c, 2)
    across = lax.rem(c + 2, n_col)
    far = lax.rem(pair + 2, n_col)

    def tiles_of(number, c2, body, rows=(3, 2, 1, 0)):
        for q in rows:
            if number == 1:
                body(q)
            else:
                pl.when(q >= c2)(functools.partial(body, q))

    def hand(weights, slot, q, number, kind, c2):
        pltpu.make_async_remote_copy(
            src_ref=weights.at[slot, q],
            dst_ref=weights.at[slot, q],
            send_sem=share_sems.at[number, kind, q],
            recv_sem=shared_sems.at[number, kind, q],
            device_id=at_row(r, c2),
            device_id_type=pl.DeviceIdType.MESH,
        ).start()

    def share(weights, number):
        tiles_of(number, c, lambda q: hand(weights, c, q, number, 0, across))
        tiles_of(number, c, lambda q: hand(weights, c, q, number, 1, pair))

    def relay(weights, number, rows=(3, 2, 1, 0)):
        def pass_on(q):
            drain(weights.at[across, q], shared_sems.at[number, 0, q])
            hand(weights, across, q, number, 2, pair)

        tiles_of(number, across, pass_on, rows)

    def settle(weights, number):
        tiles_of(number, pair, lambda q: drain(weights.at[0, q], shared_sems.at[number, 1, q]))
        tiles_of(number, far, lambda q: drain(weights.at[0, q], shared_sems.at[number, 2, q]))

    def conclude(weights, number):
        for kind, slot in enumerate((c, c, across)):
            tiles_of(
                number, slot, lambda q: drain(weights.at[0, q], share_sems.at[number, kind, q])
            )

    def lower(weights, c2):
        return weights[c2, c2:].reshape(-1, weights.shape[3])

    def flat(weights, c2):
        return weights[c2].reshape(-1, weights.shape[3])

    each(group, gid, lambda g2: greet(at_group(g2)))
    for k in range(ranks):
        greet(at_row((1 - front) * ranks + k, c))

    update = [sub_in[q].astype(F32) for q in range(n_col)]
    targets = [subtree_map[leaf, q * n_row + row] for q in range(n_col)]

    def own_block(block):
        return add_up(
            [
                jnp.where(target == block, value, jnp.zeros_like(value))
                for target, value in zip(targets, update)
            ]
        )

    for c2 in range(n_col):
        rhs = rc_in[c2].astype(F32)
        rhs = jnp.concatenate(
            [jnp.where(rank == k, rhs, jnp.zeros_like(rhs)) for k in range(ranks)], 1
        )
        placed = jnp.concatenate(
            [own_block(c2 * child_tile_blocks + b) for b in range(child_tile_blocks)], 1
        )
        p1_send[c2] = (rhs + placed).astype(BF16)
    for k in range(ranks):
        for q in range(n_col):
            tail_send[k, q] = own_block(sep_blocks + q * ranks + k).astype(BF16)
    pl.semaphore_wait(barrier, group - 1 + ranks)

    each(group, gid, lambda g2: push(p1_send.at[lax.div(g2, ranks)], p1_recv.at[gid], 0, at_group(g2)))

    def each_rank(body):
        each(ranks, rank, lambda k: body(k, at_row(front * ranks + k, c)))

    each_rank(lambda k, device: push(tail_send.at[k], tail_recv.at[rank], 1, device))
    each(rows_all, r, lambda r2: push(rr_in, rr_buf.at[r], 2, at_row(r2, c)))
    p1_recv[gid] = p1_send[c]
    tail_recv[rank] = tail_send[rank]
    rr_buf[r] = rr_in[...]
    loads[2].wait()
    share(root_w, 2)
    loads[0].wait()
    drain(p1_recv.at[pl.ds(0, group - 1)], recv_sems.at[0])
    x = jnp.concatenate(
        [
            add_up([p1_recv[p * ranks + k].astype(F32) for k in range(ranks)])
            for p in range(n_col)
        ],
        0,
    ).astype(BF16)
    for q in range(n_col):
        p2_send[q] = contract(x, child_w[c, q], 1, 1).astype(BF16)

    each(group, gid, lambda g2: push(p2_send.at[lax.div(g2, ranks)], p2_recv.at[gid], 3, at_group(g2)))
    p2_recv[gid] = p2_send[c]
    drain(tail_recv.at[pl.ds(0, ranks - 1)], recv_sems.at[1])
    tail = [add_up([tail_recv[k, q].astype(F32) for k in range(ranks)]) for q in range(n_col)]
    loads[1].wait()
    drain(p2_recv.at[pl.ds(0, group - 1)], recv_sems.at[3])
    forward = [
        add_up([p2_recv[c2 * ranks + k].astype(F32) for c2 in range(n_col)]).astype(BF16)
        for k in range(ranks)
    ]
    y = jnp.concatenate([piece.astype(F32) for piece in forward], 1).astype(BF16)
    for q in range(n_col):
        z = contract(y, off_w[c, q], 1, 1).astype(BF16)
        for p in range(n_col):
            p3_send[p, q] = z[p * panel : (p + 1) * panel]

    each(n_col, c, lambda c2: push(p3_send.at[c2], p3_recv.at[c], 4, at_row(r, c2)))
    p3_recv[c] = p3_send[c]
    own = add_up([p2_recv[c2 * ranks + rank].astype(F32) for c2 in range(n_col)])
    fw_send[...] = own.astype(BF16).reshape(fw_send.shape)
    each(n_col, c, lambda c2: push(fw_send.at[c2], fw_recv.at[c], 6, at_row(r, c2)))
    fw_recv[c] = fw_send[c]
    drain(p3_recv.at[pl.ds(0, n_col - 1)], recv_sems.at[4])
    for q in range(n_col):
        total = add_up([p3_recv[c2, q].astype(F32) for c2 in range(n_col)])
        pass_send[q] = (tail[q] - total).astype(BF16)

    each(rows_all, r, lambda r2: push(pass_send, pass_buf.at[pl.ds(r * n_col, n_col)], 5, at_row(r2, c)))
    pass_buf[pl.ds(r * n_col, n_col)] = pass_send[...]
    relay(root_w, 2, (3, 2, 1, 0))
    share(off_w, 1)
    targets = [[child_map[f, j] for j in range(child_map.shape[1])] for f in range(2)]

    def place_of(f, block):
        place = -1
        for j, target in enumerate(targets[f]):
            source = (f * ranks + j % ranks) * n_col + j // ranks
            place = jnp.where(target == block, source, place)
        return place

    places = [[place_of(f, b) for f in range(2)] for b in range(root_tile_blocks * n_col)]
    drain(rr_buf.at[pl.ds(0, rows_all - 1)], recv_sems.at[2])
    x = jnp.concatenate(
        [rr_buf[k].reshape(right, sep).astype(F32) for k in range(rows_all)], 1
    )
    drain(pass_buf.at[pl.ds(0, (rows_all - 1) * n_col)], recv_sems.at[5])

    def rows_of(values):
        return jnp.concatenate(values, 0)

    def passed(block):
        total = None
        for f in range(2):
            place = places[block][f]
            value = pass_buf[jnp.maximum(place, 0)].astype(F32)
            value = jnp.where(place >= 0, value, jnp.zeros_like(value))
            total = value if total is None else total + value
        return total

    x = x + jnp.concatenate(
        [
            rows_of([passed(q * root_tile_blocks + b) for q in range(n_col)])
            for b in range(root_tile_blocks)
        ],
        1,
    )
    x = x.astype(BF16)
    settle(root_w, 2)
    terms = []
    for c2 in range(n_col):
        term = contract(x[c2 * panel : (c2 + 1) * panel], lower(root_w, c2), 1, 1)
        if c2 > 0:
            term = jnp.concatenate([jnp.zeros((panel, c2 * sep), F32), term], 1)
        terms.append(term)
    root_forward = add_up(terms)
    for c2 in range(n_col):
        total = contract(root_forward[:, c2 * sep :].astype(BF16), lower(root_w, c2), 1, 0)
        for r2 in range(rows_all):
            p5_send[r2, c2] = total[:, r2 * sep : (r2 + 1) * sep].astype(BF16)

    each(rows_all, r, lambda r2: push(p5_send.at[r2], p5_recv.at[r], 7, at_row(r2, c)))
    p5_recv[r] = p5_send[r]
    share(child_w, 0)
    drain(p5_recv.at[pl.ds(0, rows_all - 1)], recv_sems.at[7])
    for q in range(n_col):
        total = add_up([p5_recv[k, q].astype(F32) for k in range(rows_all)])
        root_out[q] = total
        sr_send[q] = total.astype(BF16)

    each(rows_all, r, lambda r2: push(sr_send, sr_recv.at[r], 8, at_row(r2, c)))
    sr_recv[r] = sr_send[...]
    relay(off_w, 1)
    drain(sr_recv.at[pl.ds(0, rows_all - 1)], recv_sems.at[8])
    x = jnp.concatenate(
        [sr_recv[k].reshape(right, sep).astype(F32) for k in range(rows_all)], 1
    ).astype(BF16)
    for q in range(n_col):
        for b in range(root_tile_blocks):
            blocks[sep_blocks + q * root_tile_blocks + b] = x[
                q * panel : (q + 1) * panel, b * BLOCK_ROWS : (b + 1) * BLOCK_ROWS
            ]
    known = jnp.concatenate(
        [blocks[sep_blocks + child_map[front, q * ranks + rank]] for q in range(n_col)], 1
    )
    settle(off_w, 1)
    for c2 in range(n_col):
        total = contract(known, flat(off_w, c2), 1, 0)
        for k in range(ranks):
            p7_send[k, c2] = total[:, k * sep : (k + 1) * sep].astype(BF16)

    each_rank(lambda k, device: push(p7_send.at[k], p7_recv.at[rank], 9, device))
    p7_recv[rank] = p7_send[rank]
    relay(child_w, 0)
    drain(fw_recv.at[pl.ds(0, n_col - 1)], recv_sems.at[6])
    drain(p7_recv.at[pl.ds(0, ranks - 1)], recv_sems.at[9])
    back = []
    for q in range(n_col):
        total = add_up([p7_recv[k, q].astype(F32) for k in range(ranks)])
        back.append(fw_recv[q].astype(F32) - total)
    back = jnp.concatenate(back, 1)
    settle(child_w, 0)
    for c2 in range(n_col):
        total = contract(back[:, c2 * sep :].astype(BF16), lower(child_w, c2), 1, 0)
        p8_send[c2] = total.astype(BF16)

    each_rank(lambda k, device: push(p8_send, p8_recv.at[rank], 10, device))
    p8_recv[rank] = p8_send[...]
    drain(p8_recv.at[pl.ds(0, ranks - 1)], recv_sems.at[10])
    for q in range(n_col):
        total = add_up([p8_recv[k, q].astype(F32) for k in range(ranks)])
        for k in range(ranks):
            pieces[q, k] = total[:, k * sep : (k + 1) * sep]
        child_out[q] = pieces[q, rank]
        total = total.astype(BF16)
        for b in range(child_tile_blocks):
            blocks[q * child_tile_blocks + b] = total[:, b * BLOCK_ROWS : (b + 1) * BLOCK_ROWS]
    for q in range(n_col):
        block = subtree_map[leaf, q * n_row + row]
        known_block = sep_blocks + child_map[front, jnp.maximum(block - sep_blocks, 0)]
        leaf_out[q] = blocks[jnp.where(block < sep_blocks, block, known_block)]

    drain(p1_recv.at[pl.ds(0, group - 1)], send_sems.at[0])
    drain(tail_recv.at[pl.ds(0, ranks - 1)], send_sems.at[1])
    drain(rr_buf.at[pl.ds(0, rows_all - 1)], send_sems.at[2])
    drain(p2_recv.at[pl.ds(0, group - 1)], send_sems.at[3])
    drain(p3_recv.at[pl.ds(0, n_col - 1)], send_sems.at[4])
    drain(pass_buf.at[pl.ds(0, (rows_all - 1) * n_col)], send_sems.at[5])
    drain(fw_recv.at[pl.ds(0, n_col - 1)], send_sems.at[6])
    drain(p5_recv.at[pl.ds(0, rows_all - 1)], send_sems.at[7])
    drain(sr_recv.at[pl.ds(0, rows_all - 1)], send_sems.at[8])
    drain(p7_recv.at[pl.ds(0, ranks - 1)], send_sems.at[9])
    drain(p8_recv.at[pl.ds(0, ranks - 1)], send_sems.at[10])
    for number, weights in enumerate((child_w, off_w, root_w)):
        conclude(weights, number)


def fused(
    rhs_root, rhs_child, subtree_update, inv_root, inv_child, off_child, child_map, subtree_map
):
    n_col = lax.axis_size("col")
    n_row = lax.axis_size("row")
    n_leaf = lax.axis_size("leaf")
    panel = rhs_child.shape[0]
    right = panel * n_col
    sep = rhs_child.shape[2]
    ranks = n_row * (n_leaf // 2)
    rows_all = n_leaf * n_row
    group = ranks * n_col
    root_width = inv_root.shape[2]
    child_width = inv_child.shape[2]
    sep_blocks = child_width * n_col // BLOCK_ROWS
    root_blocks = root_width * n_col // BLOCK_ROWS

    def turn(array):
        return array.transpose(1, 0, 2)

    smem = pl.BlockSpec(memory_space=pltpu.SMEM)
    vmem = pl.BlockSpec(memory_space=pltpu.VMEM)
    hbm = pl.BlockSpec(memory_space=pl.ANY)
    buffer = lambda *shape: pltpu.VMEM(shape, BF16)
    outs = pl.pallas_call(
        functools.partial(solve_kernel, (n_leaf, n_row, n_col)),
        out_shape=(
            jax.ShapeDtypeStruct((n_col, panel, sep), F32),
            jax.ShapeDtypeStruct((n_col, panel, sep), F32),
            jax.ShapeDtypeStruct((n_col, panel, BLOCK_ROWS), BF16),
        ),
        in_specs=[smem] * 2 + [vmem] * 3 + [hbm] * 3,
        out_specs=(vmem, vmem, vmem),
        scratch_shapes=[
            buffer(n_col, *inv_root.shape), buffer(n_col, *inv_child.shape),
            buffer(n_col, *off_child.shape),
            buffer(n_col, panel, child_width), buffer(group, panel, child_width),
            buffer(ranks, n_col, panel, BLOCK_ROWS), buffer(ranks, n_col, panel, BLOCK_ROWS),
            buffer(rows_all, n_col, panel, sep),
            buffer(n_col, right, sep), buffer(group, right, sep),
            buffer(n_col, n_col, panel, BLOCK_ROWS), buffer(n_col, n_col, panel, BLOCK_ROWS),
            buffer(n_col, panel, BLOCK_ROWS), buffer(rows_all * n_col, panel, BLOCK_ROWS),
            buffer(n_col, panel, sep), buffer(n_col, panel, sep),
            buffer(rows_all, n_col, panel, sep), buffer(rows_all, n_col, panel, sep),
            buffer(n_col, panel, sep), buffer(rows_all, n_col, panel, sep),
            buffer(ranks, n_col, panel, sep), buffer(ranks, n_col, panel, sep),
            buffer(n_col, panel, child_width), buffer(ranks, n_col, panel, child_width),
            buffer(sep_blocks + root_blocks, panel, BLOCK_ROWS),
            pltpu.VMEM((n_col, ranks, panel, sep), F32),
            pltpu.SemaphoreType.DMA((3,)),
            pltpu.SemaphoreType.DMA((11,)),
            pltpu.SemaphoreType.DMA((11,)),
            pltpu.SemaphoreType.DMA((3, 3, 4)),
            pltpu.SemaphoreType.DMA((3, 3, 4)),
        ],
        compiler_params=pltpu.CompilerParams(
            collective_id=0, has_side_effects=True, vmem_limit_bytes=32 * 1024 * 1024
        ),
    )(
        child_map, subtree_map,
        turn(subtree_update), turn(rhs_child), turn(rhs_root), inv_root, inv_child, off_child,
    )
    return tuple(turn(out) for out in outs)


def body(*arrays):
    whole_blocks = (
        lax.axis_size("leaf") == 4
        and arrays[2].shape[2] == BLOCK_ROWS
        and arrays[4].shape[2] % BLOCK_ROWS == 0
        and arrays[0].shape[0] % 16 == 0
        and arrays[0].shape[2] % 16 == 0
    )
    return (fused if whole_blocks else local)(*arrays)


def solution(mesh):
    in_specs = (
        P("col", None, ("leaf", "row")),
        P("col", None, ("leaf", "row")),
        P("col", None, ("leaf", "row")),
        P(None, ("leaf", "row"), "col"),
        P(None, ("leaf", "row"), "col"),
        P(None, ("leaf", "row"), "col"),
        P(),
        P(),
    )
    out_specs = (
        P("col", None, ("leaf", "row")),
        P("col", None, ("leaf", "row")),
        P("col", None, ("leaf", "row")),
    )
    return jax.shard_map(body, mesh=mesh, in_specs=in_specs, out_specs=out_specs, check_vma=False)
```
